32 devices in a mesh: mem: 4 (over x, core), slab: 8 (over z, y).
Axes of the slice: x: 2, y: 2, z: 4, core: 2. Of those that a mesh axis runs over, the one named last changes fastest.
Arguments:
- anomalies: bfloat16 [8, 4096, 4096], P('mem', 'slab'), may hold values from -2.390625 to 2.390625
- increment: float32 [4096, 4096], P('slab'), may hold values from -6 to 6
- spectrum: float32 [4096, 4096], P(None, 'slab'), may hold values from 0.01 to 2, as said below
Outputs:
- product: float32 [4096, 4096], P('slab')
The draws below stay inside these ranges and needn't reach their ends.
Inputs may be any that keep to these rules, and one draw needn't show every extreme that they name: spectrum[k, l] equals spectrum[(4096 - k) % 4096, (4096 - l) % 4096], and is positive.
All inputs are finite; a program needn't handle non-finite values.
Results may differ from the reference program's by a relative error of at most 0.0003.
Values sent between devices are 32-bit elements; how exact they have to be, the bound alone decides.
A program may use at most 192 MiB of HBM per device.

```python
import jax
import jax.numpy as jnp
from jax import lax

NX = 4096
NY = 4096
MEMBERS = 8


def draw_spectrum(key, part):
    logs = jax.random.uniform(key, (NX, NY), jnp.float32, jnp.log(0.05), 0.0)
    values = jnp.exp(logs)
    mirrored = jnp.roll(jnp.flip(values, (0, 1)), 1, (0, 1))
    result = 0.5 * (values + mirrored)
    return result


def shard_levels(own_key, extent, split, low, top_value):
    loudness, own = 1.0, jax.random.fold_in(own_key, 6)
    for dim, shards_of in split:
        steps = jnp.exp(jax.random.uniform(jax.random.fold_in(own, dim), (shards_of,), jnp.float32, low / len(split), top_value / len(split)))
        loudness = loudness * jnp.repeat(steps, extent[dim] // shards_of).reshape([-1 if axis == dim else 1 for axis in range(len(extent))])
    return loudness


def noise(key, shape, spread, limit, pieces=(), held_as=jnp.bfloat16):
    level = shard_levels(key, shape, pieces, -0.22, 0.18) if pieces else 1.0
    array = jax.random.normal(key, shape, jnp.float32) * spread * level
    return jnp.minimum(jnp.maximum(array, -limit), limit).astype(held_as)


def setup_inputs(seed: int = 0) -> dict:
    streams_of = jax.random.split(jax.random.key(seed), 4)
    anomalies = noise(streams_of[0], (MEMBERS, NX, NY), 0.4, 2.390625, ((0, 4), (1, 8)))
    increment = noise(streams_of[1], (NX, NY), 1.0, 6.0, ((0, 8),), jnp.float32)
    spectrum = draw_spectrum(jax.random.fold_in(streams_of[3], 71), 0)
    return {"anomalies": anomalies, "increment": increment, "spectrum": spectrum}


def reference(anomalies, increment, spectrum):
    def member_term(index, total):
        member = lax.dynamic_index_in_dim(anomalies, index, 0, keepdims=False).astype(jnp.float32)
        field = member * increment
        waves = jnp.fft.fft2(field)
        filtered = jnp.real(jnp.fft.ifft2(waves * spectrum))
        return total + member * filtered

    start = jnp.zeros((NX, NY), jnp.float32)
    return lax.fori_loop(0, MEMBERS, member_term, start)
```

```python
import functools
import math

import jax
import jax.numpy as jnp
import numpy as np
from jax import lax
from jax.experimental import pallas as pl
from jax.experimental.pallas import tpu as pltpu
from jax.sharding import PartitionSpec as P

LANES = 128


def butterflies(parts, sign):
    n = len(parts)
    if n == 1:
        return parts
    even = butterflies(parts[0::2], sign)
    odd = butterflies(parts[1::2], sign)
    low, high = [], []
    for k in range(n // 2):
        (er, ei), (pr, pi) = even[k], odd[k]
        if k == 0:
            tr, ti = pr, pi
        elif 4 * k == n:
            tr, ti = (pi, -pr) if sign < 0 else (-pi, pr)
        elif 8 * k == n:
            h = math.sqrt(0.5)
            tr, ti = ((pr + pi) * h, (pi - pr) * h) if sign < 0 else ((pr - pi) * h, (pr + pi) * h)
        elif 8 * k == 3 * n:
            h = math.sqrt(0.5)
            tr, ti = ((pi - pr) * h, -(pr + pi) * h) if sign < 0 else (-(pr + pi) * h, (pr - pi) * h)
        else:
            angle = sign * 2.0 * math.pi * k / n
            c, s = math.cos(angle), math.sin(angle)
            tr, ti = pr * c - pi * s, pr * s + pi * c
        low.append((er + tr, ei + ti))
        high.append((er - tr, ei - ti))
    return low + high


def split(x):
    hi = x.astype(jnp.bfloat16)
    return hi, (x - hi.astype(jnp.float32)).astype(jnp.bfloat16)


def dot(a, b):
    return jnp.dot(a, b, preferred_element_type=jnp.float32)


def lane_block(sign):
    idx = np.arange(LANES)
    angle = sign * 2.0 * np.pi / LANES * (idx[:, None] * idx[None, :] % LANES)
    c, s = np.cos(angle), np.sin(angle)
    return np.block([[c, s], [-s, c]])


def split_table(table):
    hi_np = np.asarray(table.astype(jnp.bfloat16), np.float64)
    return np.stack([table.astype(jnp.bfloat16), (table - hi_np).astype(jnp.bfloat16)])


def twist(first):
    a, b = np.arange(first), np.arange(LANES)
    angle = -2.0 * np.pi / (first * LANES) * (a[:, None] * b[None, :])
    return np.stack([np.cos(angle), np.sin(angle)]).astype(np.float32)


def exchange(tiles, group):
    lane = lax.broadcasted_iota(jnp.int32, tiles[0].shape, 1)
    step = 1
    while step * group < LANES:
        width = step * group
        upper = (lane & width) != 0
        out = list(tiles)
        for t in range(len(tiles)):
            if not t & step:
                a, b = tiles[t], tiles[t + step]
                out[t] = jnp.where(upper, pltpu.roll(b, width, 1), a)
                out[t + step] = jnp.where(upper, b, pltpu.roll(a, LANES - width, 1))
        tiles = out
        step *= 2
    return tiles


def lane_matmul(y, w_ref, rows, count):
    @pl.loop(0, count)
    def _(i):
        at = pl.ds(pl.multiple_of(i * rows, rows), rows)
        hi, lo = split(y[at, :])
        y[at, :] = dot(hi, w_ref[0]) + (dot(lo, w_ref[0]) + dot(hi, w_ref[1]))


def rows_forward(first, slabs, pieces, anom, incr, w_ref, tw, *rest):
    outs, (f, y) = rest[:pieces], rest[pieces:]
    block = incr.shape[0]
    group = LANES // slabs
    per_out = first // slabs // pieces

    @pl.loop(0, block // 16)
    def _(g):
        at = pl.ds(pl.multiple_of(g * 16, 16), 16)
        inc = incr[at, :]
        f[0, at, :] = anom[0, at, :].astype(jnp.float32) * inc
        f[1, at, :] = anom[1, at, :].astype(jnp.float32) * inc

    @pl.loop(0, block // 8)
    def _(g):
        at = pl.ds(pl.multiple_of(g * 8, 8), 8)
        parts = [
            (f[0, at, a * LANES:(a + 1) * LANES], f[1, at, a * LANES:(a + 1) * LANES])
            for a in range(first)
        ]
        for c, (r, i) in enumerate(butterflies(parts, -1.0)):
            tr, ti = tw[0, c:c + 1, :], tw[1, c:c + 1, :]
            to = pl.ds(pl.multiple_of(c * block + g * 8, 8), 8)
            y[to, :LANES] = r * tr - i * ti
            y[to, LANES:] = r * ti + i * tr

    lane_matmul(y, w_ref, 4 * block, first // 4)

    @pl.loop(0, block // 8)
    def _(g):
        at = pl.ds(pl.multiple_of(g * 8, 8), 8)
        for q in range(first // slabs):
            base = q % per_out * 2 * LANES
            for half in range(2):
                lanes = slice(half * LANES, (half + 1) * LANES)
                tiles = [
                    y[pl.ds(pl.multiple_of((q * slabs + c) * block + g * 8, 8), 8), lanes]
                    for c in range(slabs)
                ]
                for s, tile in enumerate(exchange(tiles, group)):
                    outs[q // per_out][s, at, base + half * LANES:base + (half + 1) * LANES] = tile


def rows_inverse(first, slabs, pieces, anom, w_ref, tw, *rest):
    ins, out, (f, y) = rest[:pieces], rest[pieces], rest[pieces + 1:]
    block = out.shape[0]
    group = LANES // slabs
    per_out = first // slabs // pieces

    @pl.loop(0, block // 8)
    def _(g):
        at = pl.ds(pl.multiple_of(g * 8, 8), 8)
        for q in range(first // slabs):
            base = q % per_out * 2 * LANES
            for half in range(2):
                lanes = slice(half * LANES, (half + 1) * LANES)
                tiles = [
                    ins[q // per_out][s, at, base + half * LANES:base + (half + 1) * LANES]
                    for s in range(slabs)
                ]
                for c, tile in enumerate(exchange(tiles, group)):
                    to = pl.ds(pl.multiple_of((q * slabs + c) * block + g * 8, 8), 8)
                    y[to, lanes] = tile

    lane_matmul(y, w_ref, 4 * block, first // 4)

    @pl.loop(0, block // 8)
    def _(g):
        at = pl.ds(pl.multiple_of(g * 8, 8), 8)
        parts = []
        for c in range(first):
            src = pl.ds(pl.multiple_of(c * block + g * 8, 8), 8)
            r, i = y[src, :LANES], y[src, LANES:]
            tr, ti = tw[0, c:c + 1, :], tw[1, c:c + 1, :]
            parts.append((r * tr + i * ti, i * tr - r * ti))
        for a, (r, i) in enumerate(butterflies(parts, 1.0)):
            f[0, at, a * LANES:(a + 1) * LANES] = r
            f[1, at, a * LANES:(a + 1) * LANES] = i

    @pl.loop(0, block // 16)
    def _(g):
        at = pl.ds(pl.multiple_of(g * 16, 16), 16)
        out[at, :] = anom[0, at, :].astype(jnp.float32) * f[0, at, :] + anom[1, at, :].astype(
            jnp.float32
        ) * f[1, at, :]


def columns(first, bands, x, spec, w_f, w_i, tw, *rest):
    outs, y = rest[:bands], rest[bands]
    rows = x.shape[1]
    deep = rows // bands

    @pl.loop(0, LANES // 8)
    def _(g):
        parts = []
        for a in range(first):
            s, r = divmod(a * LANES, rows)
            at = pl.ds(pl.multiple_of(r + g * 8, 8), 8)
            parts.append((x[s, at, :LANES], x[s, at, LANES:]))
        for c, (r, i) in enumerate(butterflies(parts, -1.0)):
            at = pl.ds(pl.multiple_of(g * 8, 8), 8)
            im = pl.ds(pl.multiple_of(LANES + g * 8, 8), 8)
            tr, ti = tw[0, c, at, :], tw[1, c, at, :]
            lanes = slice(c % 2 * LANES, (c % 2 + 1) * LANES)
            y[c // 2, at, lanes] = r * tr - i * ti
            y[c // 2, im, lanes] = r * ti + i * tr

    @pl.loop(0, first // 2)
    def _(p):
        hi, lo = split(y[p])
        z = dot(w_f[0], hi) + (dot(w_f[0], lo) + dot(w_f[1], hi))
        m = jnp.concatenate([spec[2 * p], spec[2 * p + 1]], axis=1)
        hi, lo = split(z * jnp.concatenate([m, m], axis=0))
        y[p] = dot(w_i[0], hi) + (dot(w_i[0], lo) + dot(w_i[1], hi))

    @pl.loop(0, LANES // 8)
    def _(g):
        at = pl.ds(pl.multiple_of(g * 8, 8), 8)
        im = pl.ds(pl.multiple_of(LANES + g * 8, 8), 8)
        parts = []
        for c in range(first):
            lanes = slice(c % 2 * LANES, (c % 2 + 1) * LANES)
            r, i = y[c // 2, at, lanes], y[c // 2, im, lanes]
            tr, ti = tw[0, c, at, :], tw[1, c, at, :]
            parts.append((r * tr + i * ti, i * tr - r * ti))
        for a, (r, i) in enumerate(butterflies(parts, 1.0)):
            s, row = divmod(a * LANES, rows)
            h, row = divmod(row, deep)
            to = pl.ds(pl.multiple_of(row + g * 8, 8), 8)
            outs[h][s, to, :LANES] = r
            outs[h][s, to, LANES:] = i


def per_device(slabs, anomalies, increment, spectrum):
    f32 = jnp.float32
    members, rows, cols = anomalies.shape
    total_rows, own = spectrum.shape
    first, first_x = cols // LANES, total_rows // LANES
    chunks = first // slabs
    pieces = 2 if chunks % 2 == 0 else 1
    per_out = chunks // pieces
    bands = max(1, min(4, rows // LANES))
    deep = rows // bands
    block = min(64, deep)
    width = per_out * 2 * LANES
    vmem = 60 * 2**20
    w_f, w_i = split_table(lane_block(-1.0)), split_table(lane_block(1.0))
    w_ft = split_table(lane_block(-1.0).T)
    w_it = split_table(lane_block(1.0).T)
    tw = twist(first)
    tw_x = jnp.broadcast_to(jnp.asarray(twist(first_x))[..., None], (2, first_x, LANES, LANES))
    group = LANES // slabs

    order = np.arange(own).reshape(group, chunks, slabs).transpose(1, 2, 0).reshape(-1)
    pick = np.zeros((own, own), np.float32)
    pick[order, np.arange(own)] = 1.0 / (total_rows * cols)
    spec = jnp.dot(spectrum, pick, precision=lax.Precision.HIGHEST)
    spec = spec.reshape(LANES, first_x, own).transpose(1, 0, 2)

    whole = lambda a: pl.BlockSpec(a.shape, lambda *_: (0,) * a.ndim)
    scratch = [pltpu.VMEM((2, block, cols), f32), pltpu.VMEM((first * block, 2 * LANES), f32)]
    params = lambda: pltpu.CompilerParams(vmem_limit_bytes=vmem)
    cost = lambda n: pl.CostEstimate(
        flops=n * 3000, bytes_accessed=n * 16, transcendentals=0
    )

    waves = pl.pallas_call(
        functools.partial(rows_forward, first, slabs, pieces),
        grid=(rows // block,),
        in_specs=[
            pl.BlockSpec((2, block, cols), lambda i: (0, i, 0)),
            pl.BlockSpec((block, cols), lambda i: (i, 0)),
            whole(w_f),
            whole(tw),
        ],
        out_specs=[pl.BlockSpec((slabs, block, width), lambda i: (0, i, 0))] * pieces,
        out_shape=[jax.ShapeDtypeStruct((slabs, rows, width), f32)] * pieces,
        scratch_shapes=scratch,
        compiler_params=params(),
        cost_estimate=cost(rows * cols),
    )(anomalies, increment, w_f, tw)

    filtered = []
    for p in range(pieces):
        got = lax.all_to_all(waves[p], "slab", 0, 0)
        filtered.append(
            pl.pallas_call(
                functools.partial(columns, first_x, bands),
                grid=(per_out,),
                in_specs=[
                    pl.BlockSpec((slabs, rows, 2 * LANES), lambda j: (0, 0, j)),
                    pl.BlockSpec((first_x, LANES, LANES), lambda j, p=p: (0, 0, p * per_out + j)),
                    whole(w_ft),
                    whole(w_it),
                    whole(tw_x),
                ],
                out_specs=[pl.BlockSpec((slabs, deep, 2 * LANES), lambda j: (0, 0, j))] * bands,
                out_shape=[jax.ShapeDtypeStruct((slabs, deep, width), f32)] * bands,
                scratch_shapes=[pltpu.VMEM((first_x // 2, 2 * LANES, 2 * LANES), f32)],
                compiler_params=params(),
                cost_estimate=cost(total_rows * width),
            )(got, spec, w_ft, w_it, tw_x)
        )

    done = []
    for h in range(bands):
        back = [lax.all_to_all(filtered[p][h], "slab", 0, 0) for p in range(pieces)]
        steps = deep // block
        part = pl.pallas_call(
            functools.partial(rows_inverse, first, slabs, pieces),
            grid=(steps,),
            in_specs=[
                pl.BlockSpec((2, block, cols), lambda i, h=h: (0, h * steps + i, 0)),
                whole(w_i),
                whole(tw),
            ]
            + [pl.BlockSpec((slabs, block, width), lambda i: (0, i, 0))] * pieces,
            out_specs=pl.BlockSpec((block, cols), lambda i: (i, 0)),
            out_shape=jax.ShapeDtypeStruct((deep, cols), f32),
            scratch_shapes=scratch,
            compiler_params=params(),
            cost_estimate=cost(deep * cols),
        )(anomalies, w_i, tw, *back)
        done.append(lax.psum(part, "mem"))
    return jnp.concatenate(done, axis=0)


def solution(mesh):
    placed = (P("mem", "slab", None), P("slab", None), P(None, "slab"))
    return jax.shard_map(
        functools.partial(per_device, mesh.shape["slab"]),
        mesh=mesh,
        in_specs=placed,
        out_specs=P("slab", None),
        check_vma=False,
    )
```
